512 devices in a mesh: inst: 8 (over x, core), cell: 64 (over z, y).
Axes of the slice: x: 4, y: 4, z: 16, core: 2. Of those that a mesh axis runs over, the one named last changes fastest.
Arguments:
- adjoint: float32 [16, 6, 65536], P('inst', None, 'cell'), may hold values from -6 to 6
- source: float32 [16, 6, 65536], P('inst', None, 'cell'), may hold values from -6 to 6
- jac_diag: bfloat16 [16, 6, 6, 65536], P('inst', None, None, 'cell'), may hold values from -6 to 6
- jac_face: bfloat16 [16, 4, 6, 6, 65536], P('inst', None, None, None, 'cell'), may hold values from -4 to 4
- tile_nbr: int32 [512, 4], P('cell'), may hold values from 0 to 7
- dtau: float32 [65536], P('cell'), may hold values from 0.1 to 0.5
- fringe_src: int32 [64, 64, 64], P('cell'), may hold values from 0 to 1023
- fringe_wt: float32 [64, 64, 64], P('cell'), may hold values from 0.2 to 1
- fringe_count: int32 [64, 64], P('cell'), may hold values from 0 to 64, as said below
- fringe_dst: int32 [64, 64, 64], P(None, 'cell'), may hold values from 0 to 1023
Outputs:
- updated: float32 [16, 6, 65536], P('inst', None, 'cell')
The draws below stay inside these ranges and needn't reach their ends.
Inputs may be any that keep to these rules, and one draw needn't show every extreme that they name: `fringe_count`: each group sends 64 live slots to at least one donor owner; group loads differ by up to four times.
All inputs are finite; a program needn't handle non-finite values.
Results may differ from the reference program's by a relative error of at most 0.0003.
Values sent between devices are 32-bit elements; how exact they have to be, the bound alone decides.
No kernel may reach another device: no remote copies, remote signals or barrier semaphores. Data moves between devices by JAX's collectives and lax.ppermute only.
A program may use at most 64 MiB of HBM per device.

```python
import math
import jax
import jax.numpy as jnp
from jax import lax

INSTANCES = 16
VARS = 6
FACES = 4
TILE = 128
CELLS_DEV = 1024
CAP = 64
TILES_DEV = 8
CELLS = 65536
TILES = 512
PEERS = 64


def draw_fringe_count(key, part):
    key_base = jax.random.fold_in(key, 11)
    key_heavy = jax.random.fold_in(key, 12)
    key_pick = jax.random.fold_in(key, 13)
    base = jax.random.randint(key_base, (PEERS, PEERS), 0, CAP + 1)
    heavy = jax.random.randint(key_heavy, (PEERS, 1), 1, 5)
    counts = jnp.minimum(base * heavy // 4, CAP)
    pick = jax.random.randint(key_pick, (PEERS, 1), 0, PEERS)
    column = jnp.arange(PEERS, dtype=jnp.int32)[None, :]
    return jnp.where(column == pick, CAP, counts).astype(jnp.int32)


def touch_ends(array, rng, low, high):
    longest = array.shape.index(max(array.shape))
    spots = []
    for shift in (0, 1):
        where = [jax.random.randint(jax.random.fold_in(rng, axis), (), 0, length) for axis, length in enumerate(array.shape)]
        where[longest] = (where[longest] + shift) % array.shape[longest]
        spots.append(tuple(where))
    return array.at[spots[0]].set(low).at[spots[1]].set(high)


def block_levels(own_key, dims, split, low, high):
    def one(axis_at, parts):
        draws = jax.random.uniform(jax.random.fold_in(jax.random.fold_in(own_key, 6), axis_at), (parts,), jnp.float32, low / len(split), high / len(split))
        return jnp.repeat(jnp.exp(draws), dims[axis_at] // parts).reshape((-1,) + (1,) * (len(dims) - axis_at - 1))

    factor_of = one(*split[0])
    for cut in split[1:]:
        factor_of = factor_of * one(*cut)
    return factor_of


def gaussian(rng, extent, scale, bound, pieces=(), kind=jnp.bfloat16):
    array = jax.random.normal(rng, extent, jnp.float32) * scale
    if len(pieces) > 0:
        array = block_levels(rng, extent, pieces, -0.22, 0.18) * array
    return jnp.clip(array, min=-bound, max=bound).astype(kind)


def setup_inputs(seed: int = 0) -> dict:
    streams_of = jax.random.split(jax.random.key(seed), 11)
    return {
        "adjoint": gaussian(streams_of[0], (INSTANCES, VARS, CELLS), 1.0, 6.0, ((0, 8), (2, 64)), jnp.float32),
        "source": gaussian(streams_of[1], (INSTANCES, VARS, CELLS), 1.0, 6.0, ((0, 8), (2, 64)), jnp.float32),
        "jac_diag": gaussian(streams_of[2], (INSTANCES, VARS, VARS, CELLS), 0.4, 6.0, ((0, 8), (3, 64))),
        "jac_face": gaussian(streams_of[3], (INSTANCES, FACES, VARS, VARS, CELLS), 0.25, 4.0, ((0, 8), (4, 64))),
        "tile_nbr": touch_ends(jax.random.randint(streams_of[4], (TILES, FACES), 0, TILES_DEV), jax.random.fold_in(streams_of[4], 1), 0, TILES_DEV - 1).astype(jnp.int32),
        "dtau": jnp.clip(jnp.exp(math.log(0.5) - 1.609438 * jax.random.uniform(streams_of[5], (CELLS,), jnp.float32) ** block_levels(streams_of[5], (CELLS,), ((0, 64),), -0.2, 0.2)), 0.1, 0.5),
        "fringe_src": touch_ends(jax.random.randint(streams_of[6], (PEERS, PEERS, CAP), 0, CELLS_DEV), jax.random.fold_in(streams_of[6], 1), 0, CELLS_DEV - 1).astype(jnp.int32),
        "fringe_wt": jnp.clip(0.2 + 0.8 * jax.random.uniform(streams_of[7], (PEERS, PEERS, CAP), jnp.float32) ** block_levels(streams_of[7], (PEERS, PEERS, CAP), ((0, 64),), -0.2, 0.2), 0.2, 1.0),
        "fringe_count": draw_fringe_count(jax.random.fold_in(streams_of[10], 71), 0),
        "fringe_dst": touch_ends(jax.random.randint(streams_of[9], (PEERS, PEERS, CAP), 0, CELLS_DEV), jax.random.fold_in(streams_of[9], 1), 0, CELLS_DEV - 1).astype(jnp.int32),
    }


def spectral_matrix(count):
    rows = jnp.arange(count, dtype=jnp.int32)[:, None]
    cols = jnp.arange(count, dtype=jnp.int32)[None, :]
    offset = rows - cols
    angle = offset.astype(jnp.float32) * (jnp.pi / count)
    parity = jnp.where(offset % 2 == 0, 1.0, -1.0).astype(jnp.float32)
    denom = jnp.where(offset == 0, 1.0, jnp.sin(angle))
    value = 0.25 * parity * jnp.cos(angle) / denom
    return jnp.where(offset == 0, 0.0, value).astype(jnp.float32)


def reference(adjoint, source, jac_diag, jac_face, tile_nbr, dtau, fringe_src, fringe_wt, fringe_count, fringe_dst):
    smat = spectral_matrix(INSTANCES)
    temporal = jnp.einsum("ji,jac->iac", smat, adjoint, precision=lax.Precision.HIGHEST)
    own = jnp.sum(jac_diag.astype(jnp.float32) * adjoint[:, :, None, :], axis=1)
    tiles = adjoint.reshape(INSTANCES, VARS, TILES, TILE)
    group = (jnp.arange(TILES, dtype=jnp.int32) // TILES_DEV) * TILES_DEV
    faced = jnp.zeros_like(adjoint)
    for face in range(FACES):
        neighbour = (group + tile_nbr[:, face]).astype(jnp.int32)
        near = tiles[:, :, neighbour, :].reshape(INSTANCES, VARS, CELLS)
        faced = faced + jnp.sum(jac_face[:, face].astype(jnp.float32) * near[:, :, None, :], axis=1)
    peers = jnp.arange(PEERS, dtype=jnp.int32)
    src_global = (peers[:, None, None] * CELLS_DEV + fringe_src).reshape(-1)
    dst_global = (peers[None, :, None] * CELLS_DEV + fringe_dst).reshape(-1)
    live = jnp.arange(CAP, dtype=jnp.int32)[None, None, :] < fringe_count[:, :, None]
    coef = jnp.where(live, fringe_wt, 0.0).reshape(-1)
    values = adjoint[:, :, src_global] * coef
    fringe = jnp.zeros_like(adjoint).at[:, :, dst_global].add(values)
    total = own + faced + temporal + fringe - source
    return adjoint - dtau[None, None, :] * total
```

```python
import jax
import jax.numpy as jnp
import numpy as np
from jax import lax
from jax.experimental import pallas as pl
from jax.experimental.pallas import tpu as pltpu
from jax.sharding import PartitionSpec as P

INSTANCES = 16
FACES = 4
TILE = 128
LOW = 256


def spectral_matrix(count):
    offset = np.arange(count)[:, None] - np.arange(count)[None, :]
    angle = offset.astype(np.float32) * np.float32(np.pi / count)
    parity = np.where(offset % 2 == 0, 1.0, -1.0).astype(np.float32)
    denom = np.where(offset == 0, np.float32(1.0), np.sin(angle))
    value = np.float32(0.25) * parity * np.cos(angle) / denom
    return np.where(offset == 0, 0.0, value).astype(np.float32)


def in_vmem(x):
    return pltpu.with_memory_space_constraint(x, pltpu.VMEM)


def lane_pairs(even, odd):
    return jnp.concatenate([even, odd], axis=1)


def pick_kernel(adj_ref, src_ref, wt_ref, count_ref, out_ref, table, coef_ref, lo_ref, hi_ref, pair_ref):
    nvars, inst, cells = adj_ref.shape
    peers, cap = src_ref.shape[1:]
    pairs = peers // 2
    table[:, nvars:, :] = jnp.zeros((inst, 8 - nvars, cells), jnp.float32)
    for i in range(inst):
        for a in range(nvars):
            table[i, a : a + 1, :] = adj_ref[a, i : i + 1, :]
    row = lax.broadcasted_iota(jnp.int32, (peers, peers), 0)
    col = lax.broadcasted_iota(jnp.int32, (peers, peers), 1)
    counts = jnp.sum(jnp.where(row == col, count_ref[...], 0), axis=1, keepdims=True)
    slot = lax.broadcasted_iota(jnp.int32, (peers, cap), 1)
    coef_ref[...] = jnp.where(slot < counts, wt_ref[0], 0.0)
    src = lane_pairs(src_ref[0, pl.ds(0, pairs, stride=2), :], src_ref[0, pl.ds(1, pairs, stride=2), :])
    lo_ref[...] = src & (TILE - 1)
    hi_ref[...] = src >> 7
    pair_ref[...] = lane_pairs(coef_ref[pl.ds(0, pairs, stride=2), :], coef_ref[pl.ds(1, pairs, stride=2), :])
    left = lax.broadcasted_iota(jnp.int32, (8, TILE), 1) < cap
    for pair in range(pairs):
        lo = jnp.broadcast_to(lo_ref[pair : pair + 1, :], (8, TILE))
        hi = jnp.broadcast_to(hi_ref[pair : pair + 1, :], (8, TILE))
        coef = jnp.broadcast_to(pair_ref[pair : pair + 1, :], (8, TILE))
        found = [jnp.zeros((8, TILE), jnp.float32) for _ in range(inst)]
        for tile in range(cells // TILE):
            here = hi == tile
            for i in range(inst):
                part = table[i, :, tile * TILE : (tile + 1) * TILE]
                got = jnp.take_along_axis(part, lo, axis=1, mode="promise_in_bounds")
                found[i] = jnp.where(here, got, found[i])
        first, second = found[0] * coef, found[1] * coef
        even = jnp.where(left, first, pltpu.roll(second, cap, 1))
        odd = jnp.where(left, pltpu.roll(first, cap, 1), second)
        for a in range(0, nvars, 2):
            out_ref[2 * pair, a // 2] = even[a : a + 2]
            out_ref[2 * pair + 1, a // 2] = odd[a : a + 2]


def pick(adjoint, src, wt, count):
    nvars, inst, cells = adjoint.shape
    peers, cap = src.shape[1:]
    pairs = peers // 2
    return pl.pallas_call(
        pick_kernel,
        out_shape=pltpu.VMEM((peers, nvars // 2, 2, TILE), jnp.float32),
        scratch_shapes=[
            pltpu.VMEM((inst, 8, cells), jnp.float32),
            pltpu.VMEM((peers, cap), jnp.float32),
            pltpu.VMEM((pairs, TILE), jnp.int32),
            pltpu.VMEM((pairs, TILE), jnp.int32),
            pltpu.VMEM((pairs, TILE), jnp.float32),
        ],
        name="pick",
    )(adjoint, src, wt, count)


def local_kernel(nbr_ref, first_ref, smat_ref, all_ref, adj_ref, source_ref, diag_ref, face_ref, dst_ref, acc_ref, hot_ref, mask_ref):
    nvars, inst, cells = adj_ref.shape
    sources, cap = dst_ref.shape
    pairs = sources // 2
    owners = all_ref.shape[0]
    row = lax.broadcasted_iota(jnp.int32, (inst, TILE), 0)
    mix = [[smat_ref[j, first_ref[0] + i] for i in range(inst)] for j in range(owners * inst)]
    mix = [jnp.where(row == 0, pair[0], pair[1]) for pair in mix]
    for tile in range(cells // TILE):
        span = slice(tile * TILE, (tile + 1) * TILE)
        starts = [pl.multiple_of(nbr_ref[face, tile] * TILE, TILE) for face in range(FACES)]
        for a in range(nvars):
            total = -source_ref[a, :, span]
            for b in range(nvars):
                total = total + diag_ref[b, a, :, span].astype(jnp.float32) * adj_ref[b, :, span]
            for owner in range(owners):
                for j in range(inst):
                    total = total + mix[owner * inst + j] * all_ref[owner, a, j : j + 1, span]
            acc_ref[a, :, span] = total
        for i in range(inst):
            sums = [jnp.zeros((FACES, TILE), jnp.float32) for _ in range(nvars)]
            for b in range(nvars):
                near = jnp.concatenate([adj_ref[b, i : i + 1, pl.ds(start, TILE)] for start in starts], axis=0)
                for a in range(nvars):
                    sums[a] = sums[a] + face_ref[i, b, a, :, span].astype(jnp.float32) * near
            for a in range(nvars):
                acc_ref[a, i : i + 1, span] += jnp.sum(sums[a], axis=0, keepdims=True)
    dst = lane_pairs(dst_ref[pl.ds(0, pairs, stride=2), :], dst_ref[pl.ds(1, pairs, stride=2), :])
    low = dst & (LOW - 1)
    high = dst >> 8
    values = lax.broadcasted_iota(jnp.int32, (LOW, TILE), 0)
    for pair in range(pairs):
        span = slice(pair * TILE, (pair + 1) * TILE)
        hot = jnp.where(values == low[pair : pair + 1, :], 1.0, 0.0)
        hot_ref[:, span] = hot.astype(jnp.bfloat16)
        for h in range(cells // LOW):
            same = jnp.where(jnp.broadcast_to(high[pair : pair + 1, :], (16, TILE)) == h, 1.0, 0.0)
            mask_ref[h, :, span] = same.astype(jnp.bfloat16)


def local_terms(nbr, first, smat, everyone, adjoint, source, diag, face, dst):
    cells = adjoint.shape[2]
    slots = dst.shape[0] * dst.shape[1]
    vmem = pl.BlockSpec(memory_space=pltpu.VMEM)
    return pl.pallas_call(
        local_kernel,
        in_specs=[pl.BlockSpec(memory_space=pltpu.SMEM)] * 3 + [vmem] * 6,
        out_specs=[vmem] * 3,
        out_shape=[
            pltpu.VMEM(adjoint.shape, jnp.float32),
            pltpu.VMEM((LOW, slots), jnp.bfloat16),
            pltpu.VMEM((cells // LOW, 16, slots), jnp.bfloat16),
        ],
        name="local",
    )(nbr, first, smat, everyone, adjoint, source, diag, face, dst)


def place_kernel(arrived_ref, hot_ref, mask_ref, acc_ref, adj_ref, dtau_ref, out_ref, split_ref):
    nvars, inst, cells = adj_ref.shape
    sources = arrived_ref.shape[0]
    cap = TILE // 2
    highs = mask_ref.shape[0]
    left = lax.broadcasted_iota(jnp.int32, (8, TILE), 1) < cap
    rest = jnp.zeros((8 - nvars, TILE), jnp.float32)
    for pair in range(sources // 2):
        span = slice(pair * TILE, (pair + 1) * TILE)
        even, odd = (
            jnp.concatenate([arrived_ref[2 * pair + k, a] for a in range(nvars // 2)] + [rest], axis=0) for k in (0, 1)
        )
        first = jnp.where(left, even, pltpu.roll(odd, cap, 1))
        second = jnp.where(left, pltpu.roll(even, cap, 1), odd)
        value = jnp.concatenate([first, second], axis=0)
        upper = value.astype(jnp.bfloat16)
        lower = (value - upper.astype(jnp.float32)).astype(jnp.bfloat16)
        for h in range(highs):
            mask = mask_ref[h, :, span]
            split_ref[h * 32 : h * 32 + 16, span] = upper * mask
            split_ref[h * 32 + 16 : h * 32 + 32, span] = lower * mask
    sums = lax.dot_general(
        split_ref[...], hot_ref[...], (((1,), (1,)), ((), ())), preferred_element_type=jnp.float32
    )
    for h in range(highs):
        span = slice(h * LOW, (h + 1) * LOW)
        both = sums[h * 32 : h * 32 + 16] + sums[h * 32 + 16 : h * 32 + 32]
        for a in range(nvars):
            fringe = jnp.concatenate([both[i * 8 + a : i * 8 + a + 1] for i in range(inst)], axis=0)
            total = acc_ref[a, :, span] + fringe
            out_ref[a, :, span] = adj_ref[a, :, span] - dtau_ref[:, span] * total


def place(arrived, hot, mask, acc, adjoint, dtau):
    rows = mask.shape[0] * 32
    return pl.pallas_call(
        place_kernel,
        out_shape=jax.ShapeDtypeStruct(adjoint.shape, jnp.float32),
        scratch_shapes=[pltpu.VMEM((rows, hot.shape[1]), jnp.bfloat16)],
        name="place",
    )(arrived, hot, mask, acc, adjoint, dtau)


def on_device(
    adjoint,
    source,
    jac_diag,
    jac_face,
    tile_nbr,
    dtau,
    fringe_src,
    fringe_wt,
    fringe_count,
    fringe_dst,
):
    smat = jnp.asarray(spectral_matrix(INSTANCES))
    first = (lax.axis_index("inst").astype(jnp.int32) * adjoint.shape[0]).reshape(1)
    adjoint = jnp.transpose(adjoint, (1, 0, 2))
    outgoing = pick(adjoint, fringe_src, fringe_wt, fringe_count)
    arrived = lax.all_to_all(outgoing, "cell", split_axis=0, concat_axis=0, tiled=True)
    later, _ = lax.optimization_barrier((adjoint, outgoing))
    everyone = lax.all_gather(later, "inst")
    acc, hot, mask = local_terms(
        tile_nbr.T,
        first,
        smat,
        everyone,
        later,
        jnp.transpose(source, (1, 0, 2)),
        jnp.transpose(jac_diag, (1, 2, 0, 3)),
        jnp.transpose(jac_face, (0, 2, 3, 1, 4)),
        fringe_dst[:, 0, :],
    )
    arrived, hot, mask, acc = (in_vmem(x) for x in (arrived, hot, mask, acc))
    updated = place(arrived, hot, mask, acc, adjoint, dtau[None, :])
    return jnp.transpose(updated, (1, 0, 2))


def solution(mesh):
    placed = (
        P("inst", None, "cell"),
        P("inst", None, "cell"),
        P("inst", None, None, "cell"),
        P("inst", None, None, None, "cell"),
        P("cell", None),
        P("cell"),
        P("cell", None, None),
        P("cell", None, None),
        P("cell", None),
        P(None, "cell", None),
    )
    return jax.shard_map(
        on_device, mesh=mesh, in_specs=placed, out_specs=P("inst", None, "cell"), check_vma=False
    )
```

```python
import jax
import jax.numpy as jnp
import numpy as np
from jax import lax
from jax.experimental import pallas as pl
from jax.experimental.pallas import tpu as pltpu
from jax.sharding import PartitionSpec as P

INSTANCES = 16
FACES = 4
TILE = 128
LOW = 256
CHUNKS = 4


def spectral_matrix(count):
    offset = np.arange(count)[:, None] - np.arange(count)[None, :]
    angle = offset.astype(np.float32) * np.float32(np.pi / count)
    parity = np.where(offset % 2 == 0, 1.0, -1.0).astype(np.float32)
    denom = np.where(offset == 0, np.float32(1.0), np.sin(angle))
    value = np.float32(0.25) * parity * np.cos(angle) / denom
    return np.where(offset == 0, 0.0, value).astype(np.float32)


def in_vmem(x):
    return pltpu.with_memory_space_constraint(x, pltpu.VMEM)


def lane_pairs(even, odd):
    return jnp.concatenate([even, odd], axis=1)


def pick_kernel(adj_ref, src_ref, wt_ref, count_ref, out_ref, split, coef_ref, slot_ref, pair_ref, buf, sem):
    nvars, inst, cells = adj_ref.shape
    peers, cap = src_ref.shape[1:]
    pairs = peers // 2
    highs = cells // LOW
    row = lax.broadcasted_iota(jnp.int32, (peers, peers), 0)
    col = lax.broadcasted_iota(jnp.int32, (peers, peers), 1)
    counts = jnp.sum(jnp.where(row == col, count_ref[...], 0), axis=1, keepdims=True)
    slot = lax.broadcasted_iota(jnp.int32, (peers, cap), 1)
    coef_ref[...] = jnp.where(slot < counts, wt_ref[0], 0.0)
    slot_ref[...] = lane_pairs(src_ref[0, pl.ds(0, pairs, stride=2), :], src_ref[0, pl.ds(1, pairs, stride=2), :])
    pair_ref[...] = lane_pairs(coef_ref[pl.ds(0, pairs, stride=2), :], coef_ref[pl.ds(1, pairs, stride=2), :])
    rest = jnp.zeros((8 - nvars, LOW), jnp.float32)
    for h in range(highs):
        for i in range(inst):
            value = [adj_ref[a, i : i + 1, h * LOW : (h + 1) * LOW] for a in range(nvars)]
            value = jnp.concatenate(value + [rest], axis=0)
            upper = value.astype(jnp.bfloat16)
            at = h * 32 + i * 8
            split[at : at + 8, :] = upper
            split[at + 16 : at + 24, :] = (value - upper.astype(jnp.float32)).astype(jnp.bfloat16)
    left = lax.broadcasted_iota(jnp.int32, (8, TILE), 1) < cap
    values = lax.broadcasted_iota(jnp.int32, (LOW, LOW), 0)
    copies = []
    for pair in range(0, pairs, 2):
        src = lane_pairs(slot_ref[pair : pair + 1, :], slot_ref[pair + 1 : pair + 2, :])
        coef = lane_pairs(pair_ref[pair : pair + 1, :], pair_ref[pair + 1 : pair + 2, :])
        hot = jnp.where(values == (src & (LOW - 1)), 1.0, 0.0).astype(jnp.bfloat16)
        every = jnp.dot(split[...], hot, preferred_element_type=jnp.float32)
        high = jnp.broadcast_to(src >> 8, (16, LOW))
        found = jnp.zeros((16, LOW), jnp.float32)
        for h in range(highs):
            found = jnp.where(high == h, every[h * 32 : h * 32 + 16] + every[h * 32 + 16 : h * 32 + 32], found)
        found = found * coef
        for k in range(2):
            first = found[:8, k * TILE : (k + 1) * TILE]
            second = found[8:, k * TILE : (k + 1) * TILE]
            even = jnp.where(left, first, pltpu.roll(second, cap, 1))
            odd = jnp.where(left, pltpu.roll(first, cap, 1), second)
            for a in range(0, nvars, 2):
                buf[2 * (pair + k), a // 2] = even[a : a + 2]
                buf[2 * (pair + k) + 1, a // 2] = odd[a : a + 2]
        step = peers // CHUNKS
        if (2 * pair + 4) % step == 0:
            chunk = (2 * pair + 4) // step - 1
            span = pl.ds(chunk * step, step)
            copy = pltpu.make_async_copy(buf.at[span], out_ref.at[span], sem.at[chunk])
            copy.start()
            copies.append(copy)
    for copy in copies:
        copy.wait()


def pick(adjoint, src, wt, count):
    nvars, inst, cells = adjoint.shape
    peers, cap = src.shape[1:]
    pairs = peers // 2
    chunks = (peers, nvars // 2, 2, TILE)
    return pl.pallas_call(
        pick_kernel,
        out_shape=jax.ShapeDtypeStruct(chunks, jnp.float32),
        out_specs=pl.BlockSpec(memory_space=pl.ANY),
        scratch_shapes=[
            pltpu.VMEM((cells // LOW * 32, LOW), jnp.bfloat16),
            pltpu.VMEM((peers, cap), jnp.float32),
            pltpu.VMEM((pairs, TILE), jnp.int32),
            pltpu.VMEM((pairs, TILE), jnp.float32),
            pltpu.VMEM(chunks, jnp.float32),
            pltpu.SemaphoreType.DMA((CHUNKS,)),
        ],
        name="pick",
    )(adjoint, src, wt, count)


def local_kernel(nbr_ref, first_ref, smat_ref, all_ref, adj_ref, source_ref, diag_ref, face_ref, dst_ref, dtau_ref, base_ref, step_ref, hot_ref, mask_ref, acc_ref):
    nvars, inst, cells = adj_ref.shape
    sources, cap = dst_ref.shape
    pairs = sources // 2
    owners = all_ref.shape[0]
    row = lax.broadcasted_iota(jnp.int32, (inst, TILE), 0)
    mix = [[smat_ref[j, first_ref[0] + i] for i in range(inst)] for j in range(owners * inst)]
    mix = [jnp.where(row == 0, pair[0], pair[1]) for pair in mix]
    for tile in range(cells // TILE):
        span = slice(tile * TILE, (tile + 1) * TILE)
        starts = [pl.multiple_of(nbr_ref[face, tile] * TILE, TILE) for face in range(FACES)]
        for a in range(nvars):
            total = -source_ref[a, :, span]
            for b in range(nvars):
                total = total + diag_ref[b, a, :, span].astype(jnp.float32) * adj_ref[b, :, span]
            for owner in range(owners):
                for j in range(inst):
                    total = total + mix[owner * inst + j] * all_ref[owner, a, j : j + 1, span]
            acc_ref[a, :, span] = total
        for i in range(inst):
            sums = [jnp.zeros((FACES, TILE), jnp.float32) for _ in range(nvars)]
            for b in range(nvars):
                near = jnp.concatenate([adj_ref[b, i : i + 1, pl.ds(start, TILE)] for start in starts], axis=0)
                for a in range(nvars):
                    sums[a] = sums[a] + face_ref[i, b, a, :, span].astype(jnp.float32) * near
            for a in range(nvars):
                acc_ref[a, i : i + 1, span] += jnp.sum(sums[a], axis=0, keepdims=True)
    step = dtau_ref[...]
    step_ref[...] = step
    for a in range(nvars):
        base_ref[a] = adj_ref[a] - step * acc_ref[a]
    dst = lane_pairs(dst_ref[pl.ds(0, pairs, stride=2), :], dst_ref[pl.ds(1, pairs, stride=2), :])
    low = dst & (LOW - 1)
    high = dst >> 8
    values = lax.broadcasted_iota(jnp.int32, (LOW, TILE), 0)
    for pair in range(pairs):
        span = slice(pair * TILE, (pair + 1) * TILE)
        hot = jnp.where(values == low[pair : pair + 1, :], 1.0, 0.0)
        hot_ref[:, span] = hot.astype(jnp.bfloat16)
        for h in range(cells // LOW):
            same = jnp.where(jnp.broadcast_to(high[pair : pair + 1, :], (16, TILE)) == h, 1.0, 0.0)
            mask_ref[h, :, span] = same.astype(jnp.bfloat16)


def local_terms(nbr, first, smat, everyone, adjoint, source, diag, face, dst, dtau):
    cells = adjoint.shape[2]
    slots = dst.shape[0] * dst.shape[1]
    vmem = pl.BlockSpec(memory_space=pltpu.VMEM)
    return pl.pallas_call(
        local_kernel,
        in_specs=[pl.BlockSpec(memory_space=pltpu.SMEM)] * 3 + [vmem] * 7,
        out_specs=[vmem] * 4,
        out_shape=[
            pltpu.VMEM(adjoint.shape, jnp.float32),
            pltpu.VMEM(dtau.shape, jnp.float32),
            pltpu.VMEM((LOW, slots), jnp.bfloat16),
            pltpu.VMEM((cells // LOW, 16, slots), jnp.bfloat16),
        ],
        scratch_shapes=[pltpu.VMEM(adjoint.shape, jnp.float32)],
        name="local",
    )(nbr, first, smat, everyone, adjoint, source, diag, face, dst, dtau)


def place_kernel(arrived_ref, hot_ref, mask_ref, base_ref, step_ref, out_ref, split_ref):
    nvars, inst, cells = base_ref.shape
    sources = arrived_ref.shape[0]
    cap = TILE // 2
    highs = mask_ref.shape[0]
    left = lax.broadcasted_iota(jnp.int32, (8, TILE), 1) < cap
    rest = jnp.zeros((8 - nvars, TILE), jnp.float32)
    for pair in range(sources // 2):
        span = slice(pair * TILE, (pair + 1) * TILE)
        even, odd = (
            jnp.concatenate([arrived_ref[2 * pair + k, a] for a in range(nvars // 2)] + [rest], axis=0) for k in (0, 1)
        )
        first = jnp.where(left, even, pltpu.roll(odd, cap, 1))
        second = jnp.where(left, pltpu.roll(even, cap, 1), odd)
        value = jnp.concatenate([first, second], axis=0)
        upper = value.astype(jnp.bfloat16)
        lower = (value - upper.astype(jnp.float32)).astype(jnp.bfloat16)
        for h in range(highs):
            mask = mask_ref[h, :, span]
            split_ref[h * 32 : h * 32 + 16, span] = upper * mask
            split_ref[h * 32 + 16 : h * 32 + 32, span] = lower * mask
    sums = lax.dot_general(
        split_ref[...], hot_ref[...], (((1,), (1,)), ((), ())), preferred_element_type=jnp.float32
    )
    for h in range(highs):
        span = slice(h * LOW, (h + 1) * LOW)
        both = sums[h * 32 : h * 32 + 16] + sums[h * 32 + 16 : h * 32 + 32]
        for a in range(nvars):
            fringe = jnp.concatenate([both[i * 8 + a : i * 8 + a + 1] for i in range(inst)], axis=0)
            out_ref[a, :, span] = base_ref[a, :, span] - step_ref[:, span] * fringe


def place(arrived, hot, mask, base, step):
    rows = mask.shape[0] * 32
    return pl.pallas_call(
        place_kernel,
        out_shape=jax.ShapeDtypeStruct(base.shape, jnp.float32),
        scratch_shapes=[pltpu.VMEM((rows, hot.shape[1]), jnp.bfloat16)],
        name="place",
    )(arrived, hot, mask, base, step)


def on_device(
    adjoint,
    source,
    jac_diag,
    jac_face,
    tile_nbr,
    dtau,
    fringe_src,
    fringe_wt,
    fringe_count,
    fringe_dst,
):
    smat = jnp.asarray(spectral_matrix(INSTANCES))
    first = (lax.axis_index("inst").astype(jnp.int32) * adjoint.shape[0]).reshape(1)
    adjoint = jnp.transpose(adjoint, (1, 0, 2))
    outgoing = pick(adjoint, fringe_src, fringe_wt, fringe_count)
    arrived = lax.all_to_all(outgoing, "cell", split_axis=0, concat_axis=0, tiled=True)
    later, _ = lax.optimization_barrier((adjoint, outgoing))
    everyone = lax.all_gather(later, "inst")
    base, step, hot, mask = local_terms(
        tile_nbr.T,
        first,
        smat,
        everyone,
        later,
        jnp.transpose(source, (1, 0, 2)),
        jnp.transpose(jac_diag, (1, 2, 0, 3)),
        jnp.transpose(jac_face, (0, 2, 3, 1, 4)),
        fringe_dst[:, 0, :],
        dtau[None, :],
    )
    arrived, hot, mask, base, step = (in_vmem(x) for x in (arrived, hot, mask, base, step))
    updated = place(arrived, hot, mask, base, step)
    return jnp.transpose(updated, (1, 0, 2))


def solution(mesh):
    placed = (
        P("inst", None, "cell"),
        P("inst", None, "cell"),
        P("inst", None, None, "cell"),
        P("inst", None, None, None, "cell"),
        P("cell", None),
        P("cell"),
        P("cell", None, None),
        P("cell", None, None),
        P("cell", None),
        P(None, "cell", None),
    )
    return jax.shard_map(
        on_device, mesh=mesh, in_specs=placed, out_specs=P("inst", None, "cell"), check_vma=False
    )
```

```python
import jax
import jax.numpy as jnp
import numpy as np
from jax import lax
from jax.experimental import pallas as pl
from jax.experimental.pallas import tpu as pltpu
from jax.sharding import PartitionSpec as P

INSTANCES = 16
FACES = 4
TILE = 128
LOW = 256
CHUNKS = 4
FIRST = 42
EARLY = 20
LIMIT = 12 << 20


def spectral_matrix(count):
    offset = np.arange(count)[:, None] - np.arange(count)[None, :]
    angle = offset.astype(np.float32) * np.float32(np.pi / count)
    parity = np.where(offset % 2 == 0, 1.0, -1.0).astype(np.float32)
    denom = np.where(offset == 0, np.float32(1.0), np.sin(angle))
    value = np.float32(0.25) * parity * np.cos(angle) / denom
    return np.where(offset == 0, 0.0, value).astype(np.float32)


def in_vmem(x):
    return pltpu.with_memory_space_constraint(x, pltpu.VMEM)


def in_hbm(x):
    return pltpu.with_memory_space_constraint(x, pltpu.HBM)


def lane_pairs(even, odd):
    return jnp.concatenate([even, odd], axis=1)


def fetches(sources, targets, sem):
    return [pltpu.make_async_copy(a, b, sem.at[k]) for k, (a, b) in enumerate(zip(sources, targets, strict=True))]


def pick_kernel(
    early_ref, nbr_ref, adj_ref, src_ref, wt_ref, count_ref, dtau_ref, source_hbm, diag_hbm, face_hbm, dst_hbm,
    out_ref, adj_out, step_out, acc_ref, hot_ref, mask_ref,
    source_ref, diag_ref, face_ref, dst_ref, split, coef_ref, slot_ref, pair_ref, buf, sem, local_sem,
):
    needed = (source_ref, diag_ref, face_ref, dst_ref)
    loads = fetches((source_hbm, diag_hbm, face_hbm, dst_hbm), needed, local_sem)
    early = early_ref[0] == 1

    @pl.when(early)
    def _():
        for load in loads:
            load.start()

    adj_out[...] = adj_ref[...]
    step_out[...] = dtau_ref[...]
    nvars, inst, cells = adj_ref.shape
    peers, cap = src_ref.shape[1:]
    pairs = peers // 2
    highs = cells // LOW
    row = lax.broadcasted_iota(jnp.int32, (peers, peers), 0)
    col = lax.broadcasted_iota(jnp.int32, (peers, peers), 1)
    counts = jnp.sum(jnp.where(row == col, count_ref[...], 0), axis=1, keepdims=True)
    slot = lax.broadcasted_iota(jnp.int32, (peers, cap), 1)
    coef_ref[...] = jnp.where(slot < counts, wt_ref[0], 0.0)
    slot_ref[...] = lane_pairs(src_ref[0, pl.ds(0, pairs, stride=2), :], src_ref[0, pl.ds(1, pairs, stride=2), :])
    pair_ref[...] = lane_pairs(coef_ref[pl.ds(0, pairs, stride=2), :], coef_ref[pl.ds(1, pairs, stride=2), :])
    rest = jnp.zeros((8 - nvars, LOW), jnp.float32)
    for h in range(highs):
        for i in range(inst):
            value = [adj_ref[a, i : i + 1, h * LOW : (h + 1) * LOW] for a in range(nvars)]
            value = jnp.concatenate(value + [rest], axis=0)
            upper = value.astype(jnp.bfloat16)
            at = h * 32 + i * 8
            split[at : at + 8, :] = upper
            split[at + 16 : at + 24, :] = (value - upper.astype(jnp.float32)).astype(jnp.bfloat16)
    left = lax.broadcasted_iota(jnp.int32, (8, TILE), 1) < cap
    values = lax.broadcasted_iota(jnp.int32, (LOW, LOW), 0)
    copies = []
    for pair in range(0, pairs, 2):
        one, two = ((pair + k + FIRST // 2) % pairs for k in (0, 1))
        src = lane_pairs(slot_ref[one : one + 1, :], slot_ref[two : two + 1, :])
        coef = lane_pairs(pair_ref[one : one + 1, :], pair_ref[two : two + 1, :])
        hot = jnp.where(values == (src & (LOW - 1)), 1.0, 0.0).astype(jnp.bfloat16)
        every = jnp.dot(split[...], hot, preferred_element_type=jnp.float32)
        high = jnp.broadcast_to(src >> 8, (16, LOW))
        found = jnp.zeros((16, LOW), jnp.float32)
        for h in range(highs):
            found = jnp.where(high == h, every[h * 32 : h * 32 + 16] + every[h * 32 + 16 : h * 32 + 32], found)
        found = found * coef
        for k in range(2):
            first = found[:8, k * TILE : (k + 1) * TILE]
            second = found[8:, k * TILE : (k + 1) * TILE]
            even = jnp.where(left, first, pltpu.roll(second, cap, 1))
            odd = jnp.where(left, pltpu.roll(first, cap, 1), second)
            for a in range(0, nvars, 2):
                buf[2 * (pair + k), a // 2] = even[a : a + 2]
                buf[2 * (pair + k) + 1, a // 2] = odd[a : a + 2]
        step = peers // CHUNKS
        if (2 * pair + 4) % step == 0:
            chunk = (2 * pair + 4) // step - 1
            span = pl.ds(chunk * step, step)
            copy = pltpu.make_async_copy(buf.at[span], out_ref.at[span], sem.at[chunk])
            copy.start()
            copies.append(copy)

    @pl.when(early)
    def _():
        for load in loads:
            load.wait()
        local_part(nbr_ref, adj_ref, *needed, acc_ref, hot_ref, mask_ref)

    for copy in copies:
        copy.wait()


def local_scratch(source, diag, face, dst):
    return [pltpu.VMEM(x.shape, x.dtype) for x in (source, diag, face, dst)]


def pick(early, nbr, adjoint, src, wt, count, dtau, source, diag, face, dst):
    nvars, inst, cells = adjoint.shape
    slots = dst.shape[0] * dst.shape[1]
    smem = pl.BlockSpec(memory_space=pltpu.SMEM)
    vmem = pl.BlockSpec(memory_space=pltpu.VMEM)
    hbm = pl.BlockSpec(memory_space=pltpu.HBM)
    peers, cap = src.shape[1:]
    pairs = peers // 2
    chunks = (peers, nvars // 2, 2, TILE)
    return pl.pallas_call(
        pick_kernel,
        in_specs=[smem] * 2 + [vmem] * 5 + [hbm] * 4,
        out_specs=[hbm] + [vmem] * 5,
        out_shape=[
            pltpu.HBM(chunks, jnp.float32),
            pltpu.VMEM(adjoint.shape, jnp.float32),
            pltpu.VMEM(dtau.shape, jnp.float32),
            pltpu.VMEM(adjoint.shape, jnp.float32),
            pltpu.VMEM((LOW, slots), jnp.bfloat16),
            pltpu.VMEM((cells // LOW, 16, slots), jnp.bfloat16),
        ],
        scratch_shapes=local_scratch(source, diag, face, dst)
        + [
            pltpu.VMEM((cells // LOW * 32, LOW), jnp.bfloat16),
            pltpu.VMEM((peers, cap), jnp.float32),
            pltpu.VMEM((pairs, TILE), jnp.int32),
            pltpu.VMEM((pairs, TILE), jnp.float32),
            pltpu.VMEM(chunks, jnp.float32),
            pltpu.SemaphoreType.DMA((CHUNKS,)),
            pltpu.SemaphoreType.DMA((4,)),
        ],
        compiler_params=pltpu.CompilerParams(vmem_limit_bytes=LIMIT),
        name="pick",
    )(early, nbr, adjoint, src, wt, count, dtau, source, diag, face, dst)


def local_part(nbr_ref, adj_ref, source_ref, diag_ref, face_ref, dst_ref, acc_ref, hot_ref, mask_ref):
    nvars, inst, cells = adj_ref.shape
    sources, cap = dst_ref.shape
    pairs = sources // 2
    for tile in range(cells // TILE):
        span = slice(tile * TILE, (tile + 1) * TILE)
        starts = [pl.multiple_of(nbr_ref[face, tile] * TILE, TILE) for face in range(FACES)]
        for a in range(nvars):
            total = -source_ref[a, :, span]
            for b in range(nvars):
                total = total + diag_ref[b, a, :, span].astype(jnp.float32) * adj_ref[b, :, span]
            acc_ref[a, :, span] = total
        for i in range(inst):
            sums = [jnp.zeros((FACES, TILE), jnp.float32) for _ in range(nvars)]
            for b in range(nvars):
                near = jnp.concatenate([adj_ref[b, i : i + 1, pl.ds(start, TILE)] for start in starts], axis=0)
                for a in range(nvars):
                    sums[a] = sums[a] + face_ref[i, b, a, :, span].astype(jnp.float32) * near
            for a in range(nvars):
                acc_ref[a, i : i + 1, span] += jnp.sum(sums[a], axis=0, keepdims=True)
    dst = lane_pairs(dst_ref[pl.ds(0, pairs, stride=2), :], dst_ref[pl.ds(1, pairs, stride=2), :])
    low = dst & (LOW - 1)
    high = dst >> 8
    values = lax.broadcasted_iota(jnp.int32, (LOW, TILE), 0)
    for pair in range(pairs):
        span = slice(pair * TILE, (pair + 1) * TILE)
        at = (pair + FIRST // 2) % pairs
        hot = jnp.where(values == low[at : at + 1, :], 1.0, 0.0)
        hot_ref[:, span] = hot.astype(jnp.bfloat16)
        for h in range(cells // LOW):
            same = jnp.where(jnp.broadcast_to(high[at : at + 1, :], (16, TILE)) == h, 1.0, 0.0)
            mask_ref[h, :, span] = same.astype(jnp.bfloat16)


def mix_kernel(
    early_ref, first_ref, nbr_ref, smat_ref, all_ref, adj_ref, step_ref, acc_in, hot_in, mask_in,
    source_hbm, diag_hbm, face_hbm, dst_hbm,
    base_ref, acc_ref, hot_ref, mask_ref,
    source_ref, diag_ref, face_ref, dst_ref, local_sem,
):
    del acc_in, hot_in, mask_in
    needed = (source_ref, diag_ref, face_ref, dst_ref)
    nvars, inst, cells = adj_ref.shape

    @pl.when(early_ref[0] == 0)
    def _():
        loads = fetches((source_hbm, diag_hbm, face_hbm, dst_hbm), needed, local_sem)
        for load in loads:
            load.start()
        for load in loads:
            load.wait()
        local_part(nbr_ref, adj_ref, *needed, acc_ref, hot_ref, mask_ref)

    owners = all_ref.shape[0]
    row = lax.broadcasted_iota(jnp.int32, (inst, TILE), 0)
    mix = [[smat_ref[j, first_ref[0] + i] for i in range(inst)] for j in range(owners * inst)]
    mix = [jnp.where(row == 0, pair[0], pair[1]) for pair in mix]
    for tile in range(cells // TILE):
        span = slice(tile * TILE, (tile + 1) * TILE)
        for a in range(nvars):
            total = acc_ref[a, :, span]
            for owner in range(owners):
                for j in range(inst):
                    total = total + mix[owner * inst + j] * all_ref[owner, a, j : j + 1, span]
            base_ref[a, :, span] = adj_ref[a, :, span] - step_ref[:, span] * total


def mix_terms(early, first, nbr, smat, everyone, adjoint, step, acc, hot, mask, source, diag, face, dst):
    smem = pl.BlockSpec(memory_space=pltpu.SMEM)
    vmem = pl.BlockSpec(memory_space=pltpu.VMEM)
    hbm = pl.BlockSpec(memory_space=pltpu.HBM)
    return pl.pallas_call(
        mix_kernel,
        in_specs=[smem] * 4 + [vmem] * 6 + [hbm] * 4,
        out_specs=[vmem] * 4,
        out_shape=[pltpu.VMEM(x.shape, x.dtype) for x in (acc, acc, hot, mask)],
        input_output_aliases={7: 1, 8: 2, 9: 3},
        scratch_shapes=local_scratch(source, diag, face, dst) + [pltpu.SemaphoreType.DMA((4,))],
        compiler_params=pltpu.CompilerParams(vmem_limit_bytes=LIMIT),
        name="mix",
    )(early, first, nbr, smat, everyone, adjoint, step, acc, hot, mask, source, diag, face, dst)


def place_kernel(arrived_ref, hot_ref, mask_ref, base_ref, step_ref, out_ref, split_ref):
    nvars, inst, cells = base_ref.shape
    sources = arrived_ref.shape[0]
    cap = TILE // 2
    highs = mask_ref.shape[0]
    left = lax.broadcasted_iota(jnp.int32, (8, TILE), 1) < cap
    rest = jnp.zeros((8 - nvars, TILE), jnp.float32)
    for pair in range(sources // 2):
        span = slice(pair * TILE, (pair + 1) * TILE)
        even, odd = (
            jnp.concatenate([arrived_ref[2 * pair + k, a] for a in range(nvars // 2)] + [rest], axis=0) for k in (0, 1)
        )
        first = jnp.where(left, even, pltpu.roll(odd, cap, 1))
        second = jnp.where(left, pltpu.roll(even, cap, 1), odd)
        value = jnp.concatenate([first, second], axis=0)
        upper = value.astype(jnp.bfloat16)
        lower = (value - upper.astype(jnp.float32)).astype(jnp.bfloat16)
        for h in range(highs):
            mask = mask_ref[h, :, span]
            split_ref[h * 32 : h * 32 + 16, span] = upper * mask
            split_ref[h * 32 + 16 : h * 32 + 32, span] = lower * mask
    sums = lax.dot_general(
        split_ref[...], hot_ref[...], (((1,), (1,)), ((), ())), preferred_element_type=jnp.float32
    )
    for h in range(highs):
        span = slice(h * LOW, (h + 1) * LOW)
        both = sums[h * 32 : h * 32 + 16] + sums[h * 32 + 16 : h * 32 + 32]
        for a in range(nvars):
            fringe = jnp.concatenate([both[i * 8 + a : i * 8 + a + 1] for i in range(inst)], axis=0)
            out_ref[a, :, span] = base_ref[a, :, span] - step_ref[:, span] * fringe


def place(arrived, hot, mask, base, step):
    rows = mask.shape[0] * 32
    return pl.pallas_call(
        place_kernel,
        out_shape=jax.ShapeDtypeStruct(base.shape, jnp.float32),
        scratch_shapes=[pltpu.VMEM((rows, hot.shape[1]), jnp.bfloat16)],
        compiler_params=pltpu.CompilerParams(vmem_limit_bytes=LIMIT),
        name="place",
    )(arrived, hot, mask, base, step)


def on_device(
    adjoint,
    source,
    jac_diag,
    jac_face,
    tile_nbr,
    dtau,
    fringe_src,
    fringe_wt,
    fringe_count,
    fringe_dst,
):
    smat = jnp.asarray(spectral_matrix(INSTANCES))
    first = (lax.axis_index("inst").astype(jnp.int32) * adjoint.shape[0]).reshape(1)
    early = (lax.axis_index("cell") < EARLY).astype(jnp.int32).reshape(1)
    adjoint = jnp.transpose(adjoint, (1, 0, 2))
    nbr = tile_nbr.T
    local = (
        jnp.transpose(source, (1, 0, 2)),
        jnp.transpose(jac_diag, (1, 2, 0, 3)),
        jnp.transpose(jac_face, (0, 2, 3, 1, 4)),
        fringe_dst[:, 0, :],
    )
    nbr, *local = (in_hbm(x) for x in (nbr, *local))
    picked = (in_hbm(x) for x in (adjoint, fringe_src, fringe_wt, fringe_count, dtau[None, :]))
    outgoing, near, step, acc, hot, mask = pick(
        early, nbr, *picked, *local
    )
    peers = fringe_wt.shape[1]
    order = [[(rank + FIRST) % peers for rank in range(peers)]]
    arrived = lax.all_to_all(
        outgoing, "cell", split_axis=0, concat_axis=0, axis_index_groups=order, tiled=True
    )
    later, _ = lax.optimization_barrier((adjoint, outgoing))
    everyone = lax.all_gather(later, "inst")
    near, step, acc, hot, mask, everyone = (in_vmem(x) for x in (near, step, acc, hot, mask, everyone))
    base, _, hot, mask = mix_terms(early, first, nbr, in_hbm(smat), everyone, near, step, acc, hot, mask, *local)
    arrived, hot, mask, base, step = (in_vmem(x) for x in (arrived, hot, mask, base, step))
    updated = place(arrived, hot, mask, base, step)
    return jnp.transpose(updated, (1, 0, 2))


def solution(mesh):
    placed = (
        P("inst", None, "cell"),
        P("inst", None, "cell"),
        P("inst", None, None, "cell"),
        P("inst", None, None, None, "cell"),
        P("cell", None),
        P("cell"),
        P("cell", None, None),
        P("cell", None, None),
        P("cell", None),
        P(None, "cell", None),
    )
    return jax.shard_map(
        on_device, mesh=mesh, in_specs=placed, out_specs=P("inst", None, "cell"), check_vma=False
    )
```

```python
import jax
import jax.numpy as jnp
import numpy as np
from jax import lax
from jax.experimental import pallas as pl
from jax.experimental.pallas import tpu as pltpu
from jax.sharding import PartitionSpec as P

INSTANCES = 16
FACES = 4
TILE = 128
LOW = 256
CHUNKS = 4
FIRST = 48
EARLY = 20
LIMIT = 12 << 20


def spectral_matrix(count):
    offset = np.arange(count)[:, None] - np.arange(count)[None, :]
    angle = offset.astype(np.float32) * np.float32(np.pi / count)
    parity = np.where(offset % 2 == 0, 1.0, -1.0).astype(np.float32)
    denom = np.where(offset == 0, np.float32(1.0), np.sin(angle))
    value = np.float32(0.25) * parity * np.cos(angle) / denom
    return np.where(offset == 0, 0.0, value).astype(np.float32)


def in_vmem(x):
    return pltpu.with_memory_space_constraint(x, pltpu.VMEM)


def in_hbm(x):
    return pltpu.with_memory_space_constraint(x, pltpu.HBM)


def lane_pairs(even, odd):
    return jnp.concatenate([even, odd], axis=1)


def fetches(sources, targets, sem):
    return [pltpu.make_async_copy(a, b, sem.at[k]) for k, (a, b) in enumerate(zip(sources, targets, strict=True))]


def pick_kernel(
    early_ref, nbr_ref, adj_ref, src_ref, wt_ref, count_ref, dtau_ref, source_hbm, diag_hbm, face_hbm, dst_hbm,
    out_ref, adj_out, step_out, acc_ref, hot_ref, mask_ref,
    source_ref, diag_ref, face_ref, dst_ref, split, coef_ref, slot_ref, pair_ref, buf, sem, local_sem,
):
    needed = (source_ref, diag_ref, face_ref, dst_ref)
    loads = fetches((source_hbm, diag_hbm, face_hbm, dst_hbm), needed, local_sem)
    early = early_ref[0] == 1

    @pl.when(early)
    def _():
        for load in loads:
            load.start()

    adj_out[...] = adj_ref[...]
    step_out[...] = dtau_ref[...]
    nvars, inst, cells = adj_ref.shape
    peers, cap = src_ref.shape[1:]
    pairs = peers // 2
    highs = cells // LOW
    row = lax.broadcasted_iota(jnp.int32, (peers, peers), 0)
    col = lax.broadcasted_iota(jnp.int32, (peers, peers), 1)
    counts = jnp.sum(jnp.where(row == col, count_ref[...], 0), axis=1, keepdims=True)
    slot = lax.broadcasted_iota(jnp.int32, (peers, cap), 1)
    coef_ref[...] = jnp.where(slot < counts, wt_ref[0], 0.0)
    slot_ref[...] = lane_pairs(src_ref[0, pl.ds(0, pairs, stride=2), :], src_ref[0, pl.ds(1, pairs, stride=2), :])
    pair_ref[...] = lane_pairs(coef_ref[pl.ds(0, pairs, stride=2), :], coef_ref[pl.ds(1, pairs, stride=2), :])
    rest = jnp.zeros((8 - nvars, LOW), jnp.float32)
    for h in range(highs):
        for i in range(inst):
            value = [adj_ref[a, i : i + 1, h * LOW : (h + 1) * LOW] for a in range(nvars)]
            value = jnp.concatenate(value + [rest], axis=0)
            upper = value.astype(jnp.bfloat16)
            at = h * 32 + i * 8
            split[at : at + 8, :] = upper
            split[at + 16 : at + 24, :] = (value - upper.astype(jnp.float32)).astype(jnp.bfloat16)
    left = lax.broadcasted_iota(jnp.int32, (8, TILE), 1) < cap
    values = lax.broadcasted_iota(jnp.int32, (LOW, LOW), 0)
    copies = []
    for pair in range(0, pairs, 2):
        one, two = ((pair + k + FIRST // 2) % pairs for k in (0, 1))
        src = lane_pairs(slot_ref[one : one + 1, :], slot_ref[two : two + 1, :])
        coef = lane_pairs(pair_ref[one : one + 1, :], pair_ref[two : two + 1, :])
        hot = jnp.where(values == (src & (LOW - 1)), 1.0, 0.0).astype(jnp.bfloat16)
        every = jnp.dot(split[...], hot, preferred_element_type=jnp.float32)
        high = jnp.broadcast_to(src >> 8, (16, LOW))
        found = jnp.zeros((16, LOW), jnp.float32)
        for h in range(highs):
            found = jnp.where(high == h, every[h * 32 : h * 32 + 16] + every[h * 32 + 16 : h * 32 + 32], found)
        found = found * coef
        for k in range(2):
            first = found[:8, k * TILE : (k + 1) * TILE]
            second = found[8:, k * TILE : (k + 1) * TILE]
            even = jnp.where(left, first, pltpu.roll(second, cap, 1))
            odd = jnp.where(left, pltpu.roll(first, cap, 1), second)
            for a in range(0, nvars, 2):
                buf[2 * (pair + k), a // 2] = even[a : a + 2]
                buf[2 * (pair + k) + 1, a // 2] = odd[a : a + 2]
        step = peers // CHUNKS
        if (2 * pair + 4) % step == 0:
            chunk = (2 * pair + 4) // step - 1
            span = pl.ds(chunk * step, step)
            copy = pltpu.make_async_copy(buf.at[span], out_ref.at[span], sem.at[chunk])
            copy.start()
            copies.append(copy)

    @pl.when(early)
    def _():
        for load in loads:
            load.wait()
        local_part(nbr_ref, adj_ref, *needed, acc_ref, hot_ref, mask_ref)

    for copy in copies:
        copy.wait()


def local_scratch(source, diag, face, dst):
    return [pltpu.VMEM(x.shape, x.dtype) for x in (source, diag, face, dst)]


def pick(early, nbr, adjoint, src, wt, count, dtau, source, diag, face, dst):
    nvars, inst, cells = adjoint.shape
    slots = dst.shape[0] * dst.shape[1]
    smem = pl.BlockSpec(memory_space=pltpu.SMEM)
    vmem = pl.BlockSpec(memory_space=pltpu.VMEM)
    hbm = pl.BlockSpec(memory_space=pltpu.HBM)
    peers, cap = src.shape[1:]
    pairs = peers // 2
    chunks = (peers, nvars // 2, 2, TILE)
    return pl.pallas_call(
        pick_kernel,
        in_specs=[smem] * 2 + [vmem] * 5 + [hbm] * 4,
        out_specs=[hbm] + [vmem] * 5,
        out_shape=[
            pltpu.HBM(chunks, jnp.float32),
            pltpu.VMEM(adjoint.shape, jnp.float32),
            pltpu.VMEM(dtau.shape, jnp.float32),
            pltpu.VMEM(adjoint.shape, jnp.float32),
            pltpu.VMEM((LOW, slots), jnp.bfloat16),
            pltpu.VMEM((cells // LOW, 16, slots), jnp.bfloat16),
        ],
        scratch_shapes=local_scratch(source, diag, face, dst)
        + [
            pltpu.VMEM((cells // LOW * 32, LOW), jnp.bfloat16),
            pltpu.VMEM((peers, cap), jnp.float32),
            pltpu.VMEM((pairs, TILE), jnp.int32),
            pltpu.VMEM((pairs, TILE), jnp.float32),
            pltpu.VMEM(chunks, jnp.float32),
            pltpu.SemaphoreType.DMA((CHUNKS,)),
            pltpu.SemaphoreType.DMA((4,)),
        ],
        compiler_params=pltpu.CompilerParams(vmem_limit_bytes=LIMIT),
        name="pick",
    )(early, nbr, adjoint, src, wt, count, dtau, source, diag, face, dst)


def local_part(nbr_ref, adj_ref, source_ref, diag_ref, face_ref, dst_ref, acc_ref, hot_ref, mask_ref):
    nvars, inst, cells = adj_ref.shape
    sources, cap = dst_ref.shape
    pairs = sources // 2
    for tile in range(cells // TILE):
        span = slice(tile * TILE, (tile + 1) * TILE)
        starts = [pl.multiple_of(nbr_ref[face, tile] * TILE, TILE) for face in range(FACES)]
        for a in range(nvars):
            total = -source_ref[a, :, span]
            for b in range(nvars):
                total = total + diag_ref[b, a, :, span].astype(jnp.float32) * adj_ref[b, :, span]
            acc_ref[a, :, span] = total
        for i in range(inst):
            sums = [jnp.zeros((FACES, TILE), jnp.float32) for _ in range(nvars)]
            for b in range(nvars):
                near = jnp.concatenate([adj_ref[b, i : i + 1, pl.ds(start, TILE)] for start in starts], axis=0)
                for a in range(nvars):
                    sums[a] = sums[a] + face_ref[i, b, a, :, span].astype(jnp.float32) * near
            for a in range(nvars):
                acc_ref[a, i : i + 1, span] += jnp.sum(sums[a], axis=0, keepdims=True)
    dst = lane_pairs(dst_ref[pl.ds(0, pairs, stride=2), :], dst_ref[pl.ds(1, pairs, stride=2), :])
    low = dst & (LOW - 1)
    high = dst >> 8
    values = lax.broadcasted_iota(jnp.int32, (LOW, TILE), 0)
    for pair in range(pairs):
        span = slice(pair * TILE, (pair + 1) * TILE)
        at = (pair + FIRST // 2) % pairs
        hot = jnp.where(values == low[at : at + 1, :], 1.0, 0.0)
        hot_ref[:, span] = hot.astype(jnp.bfloat16)
        for h in range(cells // LOW):
            same = jnp.where(jnp.broadcast_to(high[at : at + 1, :], (16, TILE)) == h, 1.0, 0.0)
            mask_ref[h, :, span] = same.astype(jnp.bfloat16)


def mix_kernel(
    early_ref, first_ref, nbr_ref, smat_ref, all_ref, adj_ref, step_ref, acc_in, hot_in, mask_in,
    source_hbm, diag_hbm, face_hbm, dst_hbm,
    base_ref, acc_ref, hot_ref, mask_ref,
    source_ref, diag_ref, face_ref, dst_ref, local_sem,
):
    del acc_in, hot_in, mask_in
    needed = (source_ref, diag_ref, face_ref, dst_ref)
    nvars, inst, cells = adj_ref.shape

    @pl.when(early_ref[0] == 0)
    def _():
        loads = fetches((source_hbm, diag_hbm, face_hbm, dst_hbm), needed, local_sem)
        for load in loads:
            load.start()
        for load in loads:
            load.wait()
        local_part(nbr_ref, adj_ref, *needed, acc_ref, hot_ref, mask_ref)

    owners = all_ref.shape[0]
    row = lax.broadcasted_iota(jnp.int32, (inst, TILE), 0)
    mix = [[smat_ref[j, first_ref[0] + i] for i in range(inst)] for j in range(owners * inst)]
    mix = [jnp.where(row == 0, pair[0], pair[1]) for pair in mix]
    for tile in range(cells // TILE):
        span = slice(tile * TILE, (tile + 1) * TILE)
        for a in range(nvars):
            total = acc_ref[a, :, span]
            for owner in range(owners):
                for j in range(inst):
                    total = total + mix[owner * inst + j] * all_ref[owner, a, j : j + 1, span]
            base_ref[a, :, span] = adj_ref[a, :, span] - step_ref[:, span] * total


def mix_terms(early, first, nbr, smat, everyone, adjoint, step, acc, hot, mask, source, diag, face, dst):
    smem = pl.BlockSpec(memory_space=pltpu.SMEM)
    vmem = pl.BlockSpec(memory_space=pltpu.VMEM)
    hbm = pl.BlockSpec(memory_space=pltpu.HBM)
    return pl.pallas_call(
        mix_kernel,
        in_specs=[smem] * 4 + [vmem] * 6 + [hbm] * 4,
        out_specs=[vmem] * 4,
        out_shape=[pltpu.VMEM(x.shape, x.dtype) for x in (acc, acc, hot, mask)],
        input_output_aliases={7: 1, 8: 2, 9: 3},
        scratch_shapes=local_scratch(source, diag, face, dst) + [pltpu.SemaphoreType.DMA((4,))],
        compiler_params=pltpu.CompilerParams(vmem_limit_bytes=LIMIT),
        name="mix",
    )(early, first, nbr, smat, everyone, adjoint, step, acc, hot, mask, source, diag, face, dst)


def place_kernel(arrived_ref, hot_ref, mask_ref, base_ref, step_ref, out_ref, split_ref):
    nvars, inst, cells = base_ref.shape
    sources = arrived_ref.shape[0]
    cap = TILE // 2
    highs = mask_ref.shape[0]
    left = lax.broadcasted_iota(jnp.int32, (8, TILE), 1) < cap
    rest = jnp.zeros((8 - nvars, TILE), jnp.float32)
    for pair in range(sources // 2):
        span = slice(pair * TILE, (pair + 1) * TILE)
        even, odd = (
            jnp.concatenate([arrived_ref[2 * pair + k, a] for a in range(nvars // 2)] + [rest], axis=0) for k in (0, 1)
        )
        first = jnp.where(left, even, pltpu.roll(odd, cap, 1))
        second = jnp.where(left, pltpu.roll(even, cap, 1), odd)
        value = jnp.concatenate([first, second], axis=0)
        upper = value.astype(jnp.bfloat16)
        lower = (value - upper.astype(jnp.float32)).astype(jnp.bfloat16)
        for h in range(highs):
            mask = mask_ref[h, :, span]
            split_ref[h * 32 : h * 32 + 16, span] = upper * mask
            split_ref[h * 32 + 16 : h * 32 + 32, span] = lower * mask
    sums = lax.dot_general(
        split_ref[...], hot_ref[...], (((1,), (1,)), ((), ())), preferred_element_type=jnp.float32
    )
    for h in range(highs):
        span = slice(h * LOW, (h + 1) * LOW)
        both = sums[h * 32 : h * 32 + 16] + sums[h * 32 + 16 : h * 32 + 32]
        for a in range(nvars):
            fringe = jnp.concatenate([both[i * 8 + a : i * 8 + a + 1] for i in range(inst)], axis=0)
            out_ref[a, :, span] = base_ref[a, :, span] - step_ref[:, span] * fringe


def place(arrived, hot, mask, base, step):
    rows = mask.shape[0] * 32
    return pl.pallas_call(
        place_kernel,
        out_shape=jax.ShapeDtypeStruct(base.shape, jnp.float32),
        scratch_shapes=[pltpu.VMEM((rows, hot.shape[1]), jnp.bfloat16)],
        compiler_params=pltpu.CompilerParams(vmem_limit_bytes=LIMIT),
        name="place",
    )(arrived, hot, mask, base, step)


def on_device(
    adjoint,
    source,
    jac_diag,
    jac_face,
    tile_nbr,
    dtau,
    fringe_src,
    fringe_wt,
    fringe_count,
    fringe_dst,
):
    smat = jnp.asarray(spectral_matrix(INSTANCES))
    first = (lax.axis_index("inst").astype(jnp.int32) * adjoint.shape[0]).reshape(1)
    early = (lax.axis_index("cell") < EARLY).astype(jnp.int32).reshape(1)
    adjoint = jnp.transpose(adjoint, (1, 0, 2))
    nbr = tile_nbr.T
    local = (
        jnp.transpose(source, (1, 0, 2)),
        jnp.transpose(jac_diag, (1, 2, 0, 3)),
        jnp.transpose(jac_face, (0, 2, 3, 1, 4)),
        fringe_dst[:, 0, :],
    )
    nbr, *local = (in_hbm(x) for x in (nbr, *local))
    picked = (in_hbm(x) for x in (adjoint, fringe_src, fringe_wt, fringe_count, dtau[None, :]))
    outgoing, near, step, acc, hot, mask = pick(
        early, nbr, *picked, *local
    )
    peers = fringe_wt.shape[1]
    order = [[(rank + FIRST) % peers for rank in range(peers)]]
    arrived = lax.all_to_all(
        outgoing, "cell", split_axis=0, concat_axis=0, axis_index_groups=order, tiled=True
    )
    later, _ = lax.optimization_barrier((adjoint, outgoing))
    everyone = lax.all_gather(later, "inst")
    near, step, acc, hot, mask, everyone = (in_vmem(x) for x in (near, step, acc, hot, mask, everyone))
    base, _, hot, mask = mix_terms(early, first, nbr, in_hbm(smat), everyone, near, step, acc, hot, mask, *local)
    arrived, hot, mask, base, step = (in_vmem(x) for x in (arrived, hot, mask, base, step))
    updated = place(arrived, hot, mask, base, step)
    return jnp.transpose(updated, (1, 0, 2))


def solution(mesh):
    placed = (
        P("inst", None, "cell"),
        P("inst", None, "cell"),
        P("inst", None, None, "cell"),
        P("inst", None, None, None, "cell"),
        P("cell", None),
        P("cell"),
        P("cell", None, None),
        P("cell", None, None),
        P("cell", None),
        P(None, "cell", None),
    )
    return jax.shard_map(
        on_device, mesh=mesh, in_specs=placed, out_specs=P("inst", None, "cell"), check_vma=False
    )
```

```python
import jax
import jax.numpy as jnp
import numpy as np
from jax import lax
from jax.experimental import pallas as pl
from jax.experimental.pallas import tpu as pltpu
from jax.sharding import PartitionSpec as P

INSTANCES = 16
FACES = 4
TILE = 128
LOW = 256
CHUNKS = 4
FIRST = 48
EARLY = 20
LIMIT = 12 << 20


def spectral_matrix(count):
    offset = np.arange(count)[:, None] - np.arange(count)[None, :]
    angle = offset.astype(np.float32) * np.float32(np.pi / count)
    parity = np.where(offset % 2 == 0, 1.0, -1.0).astype(np.float32)
    denom = np.where(offset == 0, np.float32(1.0), np.sin(angle))
    value = np.float32(0.25) * parity * np.cos(angle) / denom
    return np.where(offset == 0, 0.0, value).astype(np.float32)


def in_vmem(x):
    return pltpu.with_memory_space_constraint(x, pltpu.VMEM)


def in_hbm(x):
    return pltpu.with_memory_space_constraint(x, pltpu.HBM)


def lane_pairs(even, odd):
    return jnp.concatenate([even, odd], axis=1)


def fetches(sources, targets, sem):
    return [pltpu.make_async_copy(a, b, sem.at[k]) for k, (a, b) in enumerate(zip(sources, targets, strict=True))]


def pick_kernel(
    early_ref, nbr_ref, adj_ref, src_ref, wt_ref, count_ref, dtau_ref, source_hbm, diag_hbm, face_hbm, dst_hbm,
    out_ref, adj_out, step_out, acc_ref, hot_ref, mask_ref,
    source_ref, diag_ref, face_ref, dst_ref, split, coef_ref, slot_ref, pair_ref, buf, sem, local_sem,
):
    needed = (source_ref, diag_ref, face_ref, dst_ref)
    loads = fetches((source_hbm, diag_hbm, face_hbm, dst_hbm), needed, local_sem)
    early = early_ref[0] == 1

    @pl.when(early)
    def _():
        for load in loads:
            load.start()

    adj_out[...] = adj_ref[...]
    step_out[...] = dtau_ref[...]
    nvars, inst, cells = adj_ref.shape
    peers, cap = src_ref.shape[1:]
    pairs = peers // 2
    highs = cells // LOW
    row = lax.broadcasted_iota(jnp.int32, (peers, peers), 0)
    col = lax.broadcasted_iota(jnp.int32, (peers, peers), 1)
    counts = jnp.sum(jnp.where(row == col, count_ref[...], 0), axis=1, keepdims=True)
    slot = lax.broadcasted_iota(jnp.int32, (peers, cap), 1)
    coef_ref[...] = jnp.where(slot < counts, wt_ref[0], 0.0)
    slot_ref[...] = lane_pairs(src_ref[0, pl.ds(0, pairs, stride=2), :], src_ref[0, pl.ds(1, pairs, stride=2), :])
    pair_ref[...] = lane_pairs(coef_ref[pl.ds(0, pairs, stride=2), :], coef_ref[pl.ds(1, pairs, stride=2), :])
    rest = jnp.zeros((8 - nvars, LOW), jnp.float32)
    for h in range(highs):
        for i in range(inst):
            value = [adj_ref[a, i : i + 1, h * LOW : (h + 1) * LOW] for a in range(nvars)]
            value = jnp.concatenate(value + [rest], axis=0)
            upper = value.astype(jnp.bfloat16)
            at = h * 32 + i * 8
            split[at : at + 8, :] = upper
            split[at + 16 : at + 24, :] = (value - upper.astype(jnp.float32)).astype(jnp.bfloat16)
    left = lax.broadcasted_iota(jnp.int32, (8, TILE), 1) < cap
    values = lax.broadcasted_iota(jnp.int32, (LOW, LOW), 0)
    copies = []
    for pair in range(0, pairs, 2):
        one, two = ((pair + k + FIRST // 2) % pairs for k in (0, 1))
        src = lane_pairs(slot_ref[one : one + 1, :], slot_ref[two : two + 1, :])
        coef = lane_pairs(pair_ref[one : one + 1, :], pair_ref[two : two + 1, :])
        hot = jnp.where(values == (src & (LOW - 1)), 1.0, 0.0).astype(jnp.bfloat16)
        every = jnp.dot(split[...], hot, preferred_element_type=jnp.float32)
        high = jnp.broadcast_to(src >> 8, (16, LOW))
        found = jnp.zeros((16, LOW), jnp.float32)
        for h in range(highs):
            found = jnp.where(high == h, every[h * 32 : h * 32 + 16] + every[h * 32 + 16 : h * 32 + 32], found)
        found = found * coef
        for k in range(2):
            first = found[:8, k * TILE : (k + 1) * TILE]
            second = found[8:, k * TILE : (k + 1) * TILE]
            even = jnp.where(left, first, pltpu.roll(second, cap, 1))
            odd = jnp.where(left, pltpu.roll(first, cap, 1), second)
            for a in range(0, nvars, 2):
                buf[2 * (pair + k), a // 2] = even[a : a + 2]
                buf[2 * (pair + k) + 1, a // 2] = odd[a : a + 2]
        step = peers // CHUNKS
        if (2 * pair + 4) % step == 0:
            chunk = (2 * pair + 4) // step - 1
            span = pl.ds(chunk * step, step)
            copy = pltpu.make_async_copy(buf.at[span], out_ref.at[span], sem.at[chunk])
            copy.start()
            copies.append(copy)

    @pl.when(early)
    def _():
        for load in loads:
            load.wait()
        local_part(nbr_ref, adj_ref, *needed, acc_ref, hot_ref, mask_ref)

    for copy in copies:
        copy.wait()


def local_scratch(source, diag, face, dst):
    return [pltpu.VMEM(x.shape, x.dtype) for x in (source, diag, face, dst)]


def pick(early, nbr, adjoint, src, wt, count, dtau, source, diag, face, dst):
    nvars, inst, cells = adjoint.shape
    slots = dst.shape[0] * dst.shape[1]
    smem = pl.BlockSpec(memory_space=pltpu.SMEM)
    vmem = pl.BlockSpec(memory_space=pltpu.VMEM)
    hbm = pl.BlockSpec(memory_space=pltpu.HBM)
    peers, cap = src.shape[1:]
    pairs = peers // 2
    chunks = (peers, nvars // 2, 2, TILE)
    return pl.pallas_call(
        pick_kernel,
        in_specs=[smem] * 2 + [vmem] * 5 + [hbm] * 4,
        out_specs=[hbm] + [vmem] * 5,
        out_shape=[
            pltpu.HBM(chunks, jnp.float32),
            pltpu.VMEM(adjoint.shape, jnp.float32),
            pltpu.VMEM(dtau.shape, jnp.float32),
            pltpu.VMEM(adjoint.shape, jnp.float32),
            pltpu.VMEM((LOW, slots), jnp.bfloat16),
            pltpu.VMEM((cells // LOW, 16, slots), jnp.bfloat16),
        ],
        scratch_shapes=local_scratch(source, diag, face, dst)
        + [
            pltpu.VMEM((cells // LOW * 32, LOW), jnp.bfloat16),
            pltpu.VMEM((peers, cap), jnp.float32),
            pltpu.VMEM((pairs, TILE), jnp.int32),
            pltpu.VMEM((pairs, TILE), jnp.float32),
            pltpu.VMEM(chunks, jnp.float32),
            pltpu.SemaphoreType.DMA((CHUNKS,)),
            pltpu.SemaphoreType.DMA((4,)),
        ],
        compiler_params=pltpu.CompilerParams(vmem_limit_bytes=LIMIT),
        name="pick",
    )(early, nbr, adjoint, src, wt, count, dtau, source, diag, face, dst)


def local_part(nbr_ref, adj_ref, source_ref, diag_ref, face_ref, dst_ref, acc_ref, hot_ref, mask_ref):
    nvars, inst, cells = adj_ref.shape
    sources, cap = dst_ref.shape
    pairs = sources // 2
    for tile in range(cells // TILE):
        span = slice(tile * TILE, (tile + 1) * TILE)
        starts = [pl.multiple_of(nbr_ref[face, tile] * TILE, TILE) for face in range(FACES)]
        for a in range(nvars):
            total = -source_ref[a, :, span]
            for b in range(nvars):
                total = total + diag_ref[b, a, :, span].astype(jnp.float32) * adj_ref[b, :, span]
            acc_ref[a, :, span] = total
        for i in range(inst):
            sums = [jnp.zeros((FACES, TILE), jnp.float32) for _ in range(nvars)]
            for b in range(nvars):
                near = jnp.concatenate([adj_ref[b, i : i + 1, pl.ds(start, TILE)] for start in starts], axis=0)
                for a in range(nvars):
                    sums[a] = sums[a] + face_ref[i, b, a, :, span].astype(jnp.float32) * near
            for a in range(nvars):
                acc_ref[a, i : i + 1, span] += jnp.sum(sums[a], axis=0, keepdims=True)
    dst = lane_pairs(dst_ref[pl.ds(0, pairs, stride=2), :], dst_ref[pl.ds(1, pairs, stride=2), :])
    low = dst & (LOW - 1)
    high = dst >> 8
    values = lax.broadcasted_iota(jnp.int32, (LOW, TILE), 0)
    for pair in range(pairs):
        span = slice(pair * TILE, (pair + 1) * TILE)
        at = (pair + FIRST // 2) % pairs
        hot = jnp.where(values == low[at : at + 1, :], 1.0, 0.0)
        hot_ref[:, span] = hot.astype(jnp.bfloat16)
        for h in range(cells // LOW):
            same = jnp.where(jnp.broadcast_to(high[at : at + 1, :], (16, TILE)) == h, 1.0, 0.0)
            mask_ref[h, :, span] = same.astype(jnp.bfloat16)


def mix_kernel(
    early_ref, first_ref, nbr_ref, smat_ref, all_ref, adj_ref, step_ref, acc_in, hot_in, mask_in,
    source_hbm, diag_hbm, face_hbm, dst_hbm,
    base_ref, acc_ref, hot_ref, mask_ref,
    source_ref, diag_ref, face_ref, dst_ref, local_sem,
):
    del acc_in, hot_in, mask_in
    needed = (source_ref, diag_ref, face_ref, dst_ref)
    nvars, inst, cells = adj_ref.shape

    @pl.when(early_ref[0] == 0)
    def _():
        loads = fetches((source_hbm, diag_hbm, face_hbm, dst_hbm), needed, local_sem)
        for load in loads:
            load.start()
        for load in loads:
            load.wait()
        local_part(nbr_ref, adj_ref, *needed, acc_ref, hot_ref, mask_ref)

    owners = all_ref.shape[0]
    row = lax.broadcasted_iota(jnp.int32, (inst, cells), 0)
    mix = [[smat_ref[j, first_ref[0] + i] for i in range(inst)] for j in range(owners * inst)]
    mix = [jnp.where(row == 0, pair[0], pair[1]) for pair in mix]
    for a in range(nvars):
        total = acc_ref[a]
        for owner in range(owners):
            for j in range(inst):
                total = total + mix[owner * inst + j] * all_ref[owner, a, j : j + 1, :]
        base_ref[a] = adj_ref[a] - step_ref[...] * total


def mix_terms(early, first, nbr, smat, everyone, adjoint, step, acc, hot, mask, source, diag, face, dst):
    smem = pl.BlockSpec(memory_space=pltpu.SMEM)
    vmem = pl.BlockSpec(memory_space=pltpu.VMEM)
    hbm = pl.BlockSpec(memory_space=pltpu.HBM)
    return pl.pallas_call(
        mix_kernel,
        in_specs=[smem] * 4 + [vmem] * 6 + [hbm] * 4,
        out_specs=[vmem] * 4,
        out_shape=[pltpu.VMEM(x.shape, x.dtype) for x in (acc, acc, hot, mask)],
        input_output_aliases={7: 1, 8: 2, 9: 3},
        scratch_shapes=local_scratch(source, diag, face, dst) + [pltpu.SemaphoreType.DMA((4,))],
        compiler_params=pltpu.CompilerParams(vmem_limit_bytes=LIMIT),
        name="mix",
    )(early, first, nbr, smat, everyone, adjoint, step, acc, hot, mask, source, diag, face, dst)


def place_kernel(arrived_ref, hot_ref, mask_ref, base_ref, step_ref, out_ref, split_ref):
    nvars, inst, cells = base_ref.shape
    sources = arrived_ref.shape[0]
    cap = TILE // 2
    highs = mask_ref.shape[0]
    left = lax.broadcasted_iota(jnp.int32, (8, TILE), 1) < cap
    rest = jnp.zeros((8 - nvars, TILE), jnp.float32)
    for pair in range(sources // 2):
        span = slice(pair * TILE, (pair + 1) * TILE)
        even, odd = (
            jnp.concatenate([arrived_ref[2 * pair + k, a] for a in range(nvars // 2)] + [rest], axis=0) for k in (0, 1)
        )
        first = jnp.where(left, even, pltpu.roll(odd, cap, 1))
        second = jnp.where(left, pltpu.roll(even, cap, 1), odd)
        value = jnp.concatenate([first, second], axis=0)
        upper = value.astype(jnp.bfloat16)
        lower = (value - upper.astype(jnp.float32)).astype(jnp.bfloat16)
        for h in range(highs):
            mask = mask_ref[h, :, span]
            split_ref[h * 32 : h * 32 + 16, span] = upper * mask
            split_ref[h * 32 + 16 : h * 32 + 32, span] = lower * mask
    sums = lax.dot_general(
        split_ref[...], hot_ref[...], (((1,), (1,)), ((), ())), preferred_element_type=jnp.float32
    )
    for h in range(highs):
        span = slice(h * LOW, (h + 1) * LOW)
        both = sums[h * 32 : h * 32 + 16] + sums[h * 32 + 16 : h * 32 + 32]
        for a in range(nvars):
            fringe = jnp.concatenate([both[i * 8 + a : i * 8 + a + 1] for i in range(inst)], axis=0)
            out_ref[a, :, span] = base_ref[a, :, span] - step_ref[:, span] * fringe


def place(arrived, hot, mask, base, step):
    rows = mask.shape[0] * 32
    return pl.pallas_call(
        place_kernel,
        out_shape=jax.ShapeDtypeStruct(base.shape, jnp.float32),
        scratch_shapes=[pltpu.VMEM((rows, hot.shape[1]), jnp.bfloat16)],
        compiler_params=pltpu.CompilerParams(vmem_limit_bytes=LIMIT),
        name="place",
    )(arrived, hot, mask, base, step)


def on_device(
    adjoint,
    source,
    jac_diag,
    jac_face,
    tile_nbr,
    dtau,
    fringe_src,
    fringe_wt,
    fringe_count,
    fringe_dst,
):
    smat = jnp.asarray(spectral_matrix(INSTANCES))
    first = (lax.axis_index("inst").astype(jnp.int32) * adjoint.shape[0]).reshape(1)
    early = (lax.axis_index("cell") < EARLY).astype(jnp.int32).reshape(1)
    adjoint = jnp.transpose(adjoint, (1, 0, 2))
    nbr = tile_nbr.T
    local = (
        jnp.transpose(source, (1, 0, 2)),
        jnp.transpose(jac_diag, (1, 2, 0, 3)),
        jnp.transpose(jac_face, (0, 2, 3, 1, 4)),
        fringe_dst[:, 0, :],
    )
    nbr, *local = (in_hbm(x) for x in (nbr, *local))
    picked = (in_hbm(x) for x in (adjoint, fringe_src, fringe_wt, fringe_count, dtau[None, :]))
    outgoing, near, step, acc, hot, mask = pick(
        early, nbr, *picked, *local
    )
    peers = fringe_wt.shape[1]
    order = [[(rank + FIRST) % peers for rank in range(peers)]]
    arrived = lax.all_to_all(
        outgoing, "cell", split_axis=0, concat_axis=0, axis_index_groups=order, tiled=True
    )
    later, _ = lax.optimization_barrier((adjoint, outgoing))
    everyone = lax.all_gather(later, "inst")
    near, step, acc, hot, mask, everyone = (in_vmem(x) for x in (near, step, acc, hot, mask, everyone))
    base, _, hot, mask = mix_terms(early, first, nbr, in_hbm(smat), everyone, near, step, acc, hot, mask, *local)
    arrived, hot, mask, base, step = (in_vmem(x) for x in (arrived, hot, mask, base, step))
    updated = place(arrived, hot, mask, base, step)
    return jnp.transpose(updated, (1, 0, 2))


def solution(mesh):
    placed = (
        P("inst", None, "cell"),
        P("inst", None, "cell"),
        P("inst", None, None, "cell"),
        P("inst", None, None, None, "cell"),
        P("cell", None),
        P("cell"),
        P("cell", None, None),
        P("cell", None, None),
        P("cell", None),
        P(None, "cell", None),
    )
    return jax.shard_map(
        on_device, mesh=mesh, in_specs=placed, out_specs=P("inst", None, "cell"), check_vma=False
    )
```
